1024 devices in a mesh: context: 128 (over z_lo, y, core), tensor: 8 (over z_hi, x).
Axes of the slice: x: 4, y: 8, z: 16 (z_hi: 2, z_lo: 8; z = z_hi * 8 + z_lo), core: 2. Of those that a mesh axis runs over, the one named last changes fastest.
Arguments:
- query_proj: bfloat16 [16384, 4096], P('context', 'tensor'), may hold values from -6 to 6
- key_proj: bfloat16 [16384, 4096], P('context', 'tensor'), may hold values from -6 to 6
- value_proj: bfloat16 [16384, 4096], P('context', 'tensor'), may hold values from -6 to 6
- short_taps: float32 [3, 7, 4096], P(None, None, 'tensor'), may hold values from -2.4 to 2.4
- long_filter: float32 [8, 512, 16384], P('tensor', 'context'), may hold values from -1 to 1
- grad_mixed: bfloat16 [16384, 4096], P('context', 'tensor'), may hold values from -6 to 6
Outputs:
- mixed_out: bfloat16 [16384, 4096], P('context', 'tensor')
- input_grads: bfloat16 [3, 16384, 4096], P(None, 'context', 'tensor')
- filter_grad: float32 [8, 512, 16384], P('tensor', 'context')
The draws below stay inside these ranges and needn't reach their ends.
All inputs are finite; a program needn't handle non-finite values.
Results may differ from the reference program's by a relative error of at most 0.0064.
Values may be sent and summed in bfloat16 or wider, within the bound.
A program may use at most 32 MiB of HBM per device.

```python
import math
import jax
import jax.numpy as jnp
from jax import lax

D = 4096
TAPS = 7
SEQ = 16384
CH_TP = 512


def draw_long_filter(key, part):
    subkeys = jax.random.split(key, 4)
    lag_axis = jnp.arange(SEQ, dtype=jnp.float32)
    log_tau = jax.random.uniform(subkeys[0], (D,), jnp.float32, math.log(30.0), math.log(4 * SEQ))
    rough_part = jax.random.normal(subkeys[1], (D, SEQ), jnp.float32)
    positions = jax.random.randint(subkeys[2], (D, 3), 1, SEQ)
    losses = jnp.log(jax.random.uniform(subkeys[3], (D, 3), jnp.float32, 0.5, 0.8))
    log_env = -lag_axis[None, :] * jnp.exp(-log_tau)[:, None]
    for number in range(3):
        reached = lag_axis[None, :] >= positions[:, number:number + 1].astype(jnp.float32)
        log_env = log_env + jnp.where(reached, losses[:, number:number + 1], 0.0)
    envelope = jnp.exp(log_env)
    norm_scale = jnp.sqrt(jnp.sum(envelope * envelope, axis=1, keepdims=True))
    values = jnp.clip(rough_part * envelope / norm_scale, -1.0, 1.0)
    return values.reshape(D // CH_TP, CH_TP, SEQ)


def block_scale(stream_key, dims, cuts, low, largest):
    def one(position, shards_of):
        steps = jax.random.uniform(jax.random.fold_in(jax.random.fold_in(stream_key, 6), position), (shards_of,), jnp.float32, low / len(cuts), largest / len(cuts))
        return jnp.repeat(jnp.exp(steps), dims[position] // shards_of).reshape((-1,) + (1,) * (len(dims) - position - 1))

    loudness = one(*cuts[0])
    for cut in cuts[1:]:
        loudness = loudness * one(*cut)
    return loudness


def noise(own_key, extent, scale, bound, cuts=(), kind=jnp.bfloat16):
    entries = jax.random.normal(own_key, extent, jnp.float32) * scale
    if len(cuts) > 0:
        entries = block_scale(own_key, extent, cuts, -0.22, 0.18) * entries
    return jnp.clip(entries, min=-bound, max=bound).astype(kind)


def setup_inputs(seed: int = 0) -> dict:
    arg_keys = jax.random.split(jax.random.key(seed), 7)
    return {
        "query_proj": noise(arg_keys[0], (SEQ, D), 1.0, 6.0, ((0, 128), (1, 8))),
        "key_proj": noise(arg_keys[1], (SEQ, D), 1.0, 6.0, ((0, 128), (1, 8))),
        "value_proj": noise(arg_keys[2], (SEQ, D), 1.0, 6.0, ((0, 128), (1, 8))),
        "short_taps": noise(arg_keys[3], (3, TAPS, D), 0.4, 2.4, ((2, 8),), jnp.float32),
        "long_filter": draw_long_filter(jax.random.fold_in(arg_keys[6], 71), 0),
        "grad_mixed": noise(arg_keys[5], (SEQ, D), 1.0, 6.0, ((0, 128), (1, 8))),
    }


def causal_taps(series, tap_weights):
    series = series.astype(jnp.float32)
    running = jnp.zeros(series.shape, jnp.float32)
    for offset in range(TAPS):
        shifted = jnp.pad(series, ((offset, 0), (0, 0)))[:SEQ]
        running = running + tap_weights[offset][None, :] * shifted
    return running

def reverse_taps(series, tap_weights):
    series = series.astype(jnp.float32)
    running = jnp.zeros(series.shape, jnp.float32)
    for offset in range(TAPS):
        shifted = jnp.pad(series, ((0, offset), (0, 0)))[offset:]
        running = running + tap_weights[offset][None, :] * shifted
    return running

def one_block(block_data):
    gated_rows, grad_rows, filter_rows = block_data
    fft_len = 2 * SEQ
    spec_gate = jnp.fft.rfft(gated_rows, fft_len)
    spec_filter = jnp.fft.rfft(filter_rows, fft_len)
    spec_grad = jnp.fft.rfft(grad_rows, fft_len)
    long_rows = jnp.fft.irfft(spec_gate * spec_filter, fft_len)[:, :SEQ]
    back_rows = jnp.fft.irfft(jnp.conj(spec_filter) * spec_grad, fft_len)[:, :SEQ]
    corr_rows = jnp.fft.irfft(jnp.conj(spec_gate) * spec_grad, fft_len)[:, :SEQ]
    return (long_rows, back_rows, corr_rows)

def reference(query_proj, key_proj, value_proj, short_taps, long_filter, grad_mixed):
    query_f = causal_taps(query_proj, short_taps[0])
    key_f = causal_taps(key_proj, short_taps[1])
    value_f = causal_taps(value_proj, short_taps[2])
    gated = (key_f * value_f).astype(jnp.bfloat16)
    grad_f = grad_mixed.astype(jnp.float32)
    grad_long = (grad_f * query_f).astype(jnp.bfloat16)
    groups = D // CH_TP
    gated_rows = gated.astype(jnp.float32).T.reshape(groups, CH_TP, SEQ)
    grad_rows = grad_long.astype(jnp.float32).T.reshape(groups, CH_TP, SEQ)
    long_rows, back_rows, corr_rows = lax.map(one_block, (gated_rows, grad_rows, long_filter))
    long_conv = long_rows.reshape(D, SEQ).T.astype(jnp.bfloat16)
    grad_gated = back_rows.reshape(D, SEQ).T.astype(jnp.bfloat16)
    long_f = long_conv.astype(jnp.float32)
    mixed_out = (query_f * long_f).astype(jnp.bfloat16)
    grad_query_f = (grad_f * long_f).astype(jnp.bfloat16)
    gated_back = grad_gated.astype(jnp.float32)
    grad_key_f = (gated_back * value_f).astype(jnp.bfloat16)
    grad_value_f = (gated_back * key_f).astype(jnp.bfloat16)
    input_grads = jnp.stack([reverse_taps(grad_query_f, short_taps[0]), reverse_taps(grad_key_f, short_taps[1]), reverse_taps(grad_value_f, short_taps[2])]).astype(jnp.bfloat16)
    filter_grad = corr_rows * (1.0 / math.sqrt(SEQ))
    return (mixed_out, input_grads, filter_grad)
```

```python
import math

import jax
import jax.numpy as jnp
import numpy as np
from jax import lax
from jax.experimental import pallas as pl
from jax.experimental.pallas import tpu as pltpu
from jax.sharding import PartitionSpec as P

MESH = pl.DeviceIdType.MESH
F32 = jnp.float32
BF16 = jnp.bfloat16
B = 128
SEQ = B * B
PER = 4
TAPS = 7


def split_np(table):
    high = table.astype(jnp.bfloat16)
    low = (table - high.astype(np.float64)).astype(jnp.bfloat16)
    return high, low


def build_tables():
    idx = np.arange(B)
    psi = 2.0 * np.pi * idx[:, None] * (idx[None, :] + 0.25) / B
    phi = 2.0 * np.pi * (idx[:, None] + 0.25) * idx[None, :] / SEQ
    two = 2.0 * np.pi * ((idx[:, None] * idx[None, :]) % B) / B
    first = np.concatenate([np.cos(psi).T, -np.sin(psi).T], axis=0)
    first_back = np.concatenate([np.cos(psi), -np.sin(psi)], axis=1)
    cos, sin = np.cos(two), np.sin(two)
    second = np.block([[cos, -sin], [sin, cos]])
    second_back = np.block([[cos, sin], [-sin, cos]])
    first_cat = np.concatenate(split_np(first), axis=1)
    back_cat = np.concatenate(split_np(first_back), axis=0)
    perm = np.zeros((2 * B, 2 * B))
    for s in range(B // PER):
        for j in range(PER):
            perm[s * 2 * PER + j, PER * s + j] = 1.0
            perm[s * 2 * PER + PER + j, B + PER * s + j] = 1.0
    squares = np.stack(
        [first_cat, *split_np(second), *split_np(second_back), back_cat, perm.astype(jnp.bfloat16)]
    )
    twist = np.stack([np.cos(phi), -np.sin(phi)]).astype(np.float32)
    return squares, twist


SQUARES, TWIST = build_tables()


def split(value):
    high = value.astype(BF16)
    return high, (value - high.astype(F32)).astype(BF16)


def dot(a, b):
    return jnp.dot(a, b, preferred_element_type=F32)


def kernel(
    q_in, k_in, v_in, g_in, taps_in, filt_in, squares_in, twist_in,
    mixed_out, grads_out, fgrad_out,
    q_v, k_v, v_v, g_v, taps, filt, squares, twist,
    ext, ext_back, conv, halo_s, halo_r, halo2_s, halo2_r,
    pair, send1, recv1, send2, recv2, x32, y32,
    mid_hi, mid_lo, spec, prod_hi, prod_lo,
    in_sems, dma_sems,
):
    me = lax.axis_index("context")
    n = B

    loads = [
        pltpu.make_async_copy(src, dst, in_sems.at[i])
        for i, (src, dst) in enumerate(
            [
                (q_in, q_v), (k_in, k_v), (v_in, v_v), (taps_in, taps),
                (g_in, g_v), (filt_in, filt), (squares_in, squares), (twist_in, twist),
            ]
        )
    ]
    for load in loads:
        load.start()

    barrier = pltpu.get_barrier_semaphore()

    @pl.loop(1, n)
    def _(i):
        pl.semaphore_signal(
            barrier, inc=1, device_id={"context": lax.rem(me + i, n)}, device_id_type=MESH
        )

    def exchange(src, dst, send_sem, recv_sem):
        @pl.loop(1, n)
        def _(i):
            peer = lax.rem(me + i, n)
            pltpu.make_async_remote_copy(
                src_ref=src.at[peer], dst_ref=dst.at[me], send_sem=send_sem, recv_sem=recv_sem,
                device_id={"context": peer}, device_id_type=MESH,
            ).start()

        dst[pl.ds(me, 1)] = src[pl.ds(me, 1)]

    def all_of(src, dst, send_sem, recv_sem):
        return pltpu.make_async_remote_copy(
            src_ref=src.at[pl.ds(0, n - 1)], dst_ref=dst.at[pl.ds(0, n - 1)],
            send_sem=send_sem, recv_sem=recv_sem,
            device_id={"context": lax.rem(me + 1, n)}, device_id_type=MESH,
        )

    def halo_copy(src, dst, send_sem, recv_sem, step):
        return pltpu.make_async_remote_copy(
            src_ref=src, dst_ref=dst, send_sem=send_sem, recv_sem=recv_sem,
            device_id={"context": lax.rem(me + step + n, n)}, device_id_type=MESH,
        )

    for load in loads[:4]:
        load.wait()
    for a, src in enumerate((q_v, k_v, v_v)):
        ext[a, 0:8, :] = jnp.zeros((8, ext.shape[2]), F32)
        halo_s[a] = src[B - 16 : B, :][8:16]

    loads[4].wait()

    def short(a, first_row, rows, cols):
        acc = taps[a, 0:1, cols] * ext[a, 8 + first_row : 8 + first_row + rows, cols]
        for j in range(1, TAPS):
            start = 8 + first_row - j
            acc = acc + taps[a, j : j + 1, cols] * ext[a, start : start + rows, cols]
        return acc

    def gate(first_row, rows, tile):
        cols = pl.ds(pl.multiple_of(tile * B, B), B)
        out = []
        for a in range(3):
            value = short(a, first_row, rows, cols)
            conv[a, first_row : first_row + rows, cols] = value
            out.append(value)
        here = slice(first_row, first_row + rows)
        wide = pl.multiple_of(tile * 2 * B, 2 * B)
        pair[here, pl.ds(wide, B)] = (out[1] * out[2]).astype(BF16)
        pair[here, pl.ds(wide + B, B)] = (g_v[here, cols].astype(F32) * out[0]).astype(BF16)

    @pl.loop(0, 4)
    def _(tile):
        cols = pl.ds(pl.multiple_of(tile * B, B), B)
        for a, src in enumerate((q_v, k_v, v_v)):
            ext[a, 8 : 8 + B, cols] = src[:, cols].astype(F32)
        for first_row in range(0, B, 32):
            gate(first_row, 32, tile)

    for load in loads[5:]:
        load.wait()
    tw_re, tw_im = twist[0], twist[1]

    def put_mid(block, stage):
        re, im = stage[:B], stage[B:]
        rows = pl.ds(pl.multiple_of(block * B, B), B)
        for half, value in ((0, re * tw_re - im * tw_im), (1, re * tw_im + im * tw_re)):
            high, low = split(value)
            mid_hi[rows, half * B : half * B + B] = high
            mid_lo[rows, half * B : half * B + B] = low

    def second_stage(chunk):
        rows = pl.ds(pl.multiple_of(chunk * 2 * B, 2 * B), 2 * B)
        high = mid_hi[rows, :]
        spec[rows, :] = dot(high, squares[1]) + dot(mid_lo[rows, :], squares[1]) + dot(high, squares[2])

    @pl.loop(0, PER // 2)
    def _(p):
        rows = [filt[pl.ds(2 * p + i, B, stride=PER), :] for i in range(2)]
        high, low = split(jnp.concatenate(rows, axis=1))
        first = squares[0]
        stage = dot(first, jnp.concatenate([high, high], axis=0)) + dot(first[:, :B], low)
        for i in range(2):
            put_mid(8 + 2 * p + i, stage[:, i * B : i * B + B])
        second_stage(4 + p)

    pl.semaphore_wait(barrier, n - 1)
    halo1 = halo_copy(halo_s, halo_r, dma_sems.at[0], dma_sems.at[1], 1)

    @pl.when(me < n - 1)
    def _():
        halo1.start()

    @pl.when(me > 0)
    def _():
        halo1.wait_recv()
        for a in range(3):
            ext[a, 0:8, :] = halo_r[a].astype(F32)

    @pl.loop(0, 4)
    def _(tile):
        gate(0, 16, tile)
        wide = pl.multiple_of(tile * 2 * B, 2 * B)
        rows = lax.dot_general(
            squares[6], pair[:, pl.ds(wide, 2 * B)], (((1,), (1,)), ((), ())),
            preferred_element_type=F32,
        )
        send1[pl.ds(pl.multiple_of(tile * 32, 32), 32)] = rows.reshape(32, 8, B).astype(BF16)

    exchange(send1, recv1, dma_sems.at[2], dma_sems.at[3])
    all1 = all_of(send1, recv1, dma_sems.at[2], dma_sems.at[3])
    all1.wait_recv()

    x32[...] = recv1[...].astype(F32).reshape(8 * B, B)

    @pl.loop(0, 4)
    def _(p):
        rows = [x32[pl.ds(2 * p + i, B, stride=8), :].astype(BF16) for i in range(2)]
        signal = jnp.concatenate(rows, axis=1)
        stage = dot(squares[0], jnp.concatenate([signal, signal], axis=0))
        for i in range(2):
            put_mid(2 * p + i, stage[:, i * B : i * B + B])
        second_stage(p)

    def put_prod(block, re, im):
        rows = pl.ds(pl.multiple_of(block * B, B), B)
        for half, value in ((0, re), (1, im)):
            high, low = split(value)
            prod_hi[rows, half * B : half * B + B] = high
            prod_lo[rows, half * B : half * B + B] = low

    def spectrum(block):
        rows = pl.ds(pl.multiple_of(block * B, B), B)
        return spec[rows, 0:B], spec[rows, B : 2 * B]

    @pl.loop(0, PER)
    def _(c):
        x_re, x_im = spectrum(c)
        h_re, h_im = spectrum(8 + c)
        put_prod(c, x_re * h_re - x_im * h_im, x_re * h_im + x_im * h_re)
        g_re, g_im = spectrum(4 + c)
        put_prod(4 + c, h_re * g_re + h_im * g_im, h_re * g_im - h_im * g_re)

    def back(chunk, scale):
        rows = pl.ds(pl.multiple_of(chunk * 2 * B, 2 * B), 2 * B)
        high = prod_hi[rows, :]
        mid = dot(high, squares[3]) + dot(prod_lo[rows, :], squares[3]) + dot(high, squares[4])
        mid = mid * scale
        sides = []
        for i in range(2):
            re, im = mid[i * B : i * B + B, :B], mid[i * B : i * B + B, B:]
            sides.append(
                jnp.concatenate([re * tw_re + im * tw_im, im * tw_re - re * tw_im], axis=0)
            )
        high, low = split(jnp.concatenate(sides, axis=1))
        both = dot(squares[5], high)
        return both[:B] + both[B:] + dot(squares[5, 0:B, :], low)

    @pl.loop(0, 4)
    def _(p):
        result = back(p, 1.0 / SEQ)
        for i in range(2):
            y32[pl.ds(2 * p + i, B, stride=8), :] = result[:, i * B : i * B + B]

    send2[...] = y32[...].reshape(B, 8, B).astype(BF16)
    exchange(send2, recv2, dma_sems.at[4], dma_sems.at[5])

    @pl.loop(0, PER)
    def _(c):
        x_re, x_im = spectrum(c)
        g_re, g_im = spectrum(4 + c)
        put_prod(8 + c, x_re * g_re + x_im * g_im, x_re * g_im - x_im * g_re)

    @pl.loop(0, PER // 2)
    def _(p):
        result = back(4 + p, 1.0 / (SEQ * math.sqrt(SEQ)))
        for i in range(2):
            fgrad_out[pl.ds(2 * p + i, B, stride=PER), :] = result[:, i * B : i * B + B]

    for a in range(3):
        ext_back[a, B : B + 8, :] = jnp.zeros((8, ext_back.shape[2]), F32)
    all2 = all_of(send2, recv2, dma_sems.at[4], dma_sems.at[5])
    all2.wait_recv()

    @pl.loop(0, 4)
    def _(tile):
        cols = pl.ds(pl.multiple_of(tile * B, B), B)
        arrived = recv2[pl.ds(pl.multiple_of(tile * 32, 32), 32)].astype(F32).reshape(2 * B, B)
        rows = dot(arrived.T.astype(BF16), squares[6])
        long, gated_back = rows[:, :B], rows[:, B:]
        mixed_out[:, cols] = (conv[0, :, cols] * long).astype(BF16)
        for a, value in (
            (0, g_v[:, cols].astype(F32) * long),
            (1, gated_back * conv[2, :, cols]),
            (2, gated_back * conv[1, :, cols]),
        ):
            rounded = value.astype(BF16)
            ext_back[a, 0:B, cols] = rounded.astype(F32)
            halo2_s[a, :, cols] = rounded[0:16][0:8]

    halo2 = halo_copy(halo2_s, halo2_r, dma_sems.at[6], dma_sems.at[7], -1)

    @pl.when(me > 0)
    def _():
        halo2.start()

    def reverse(a, first_row, rows, cols):
        acc = taps[a, 0:1, cols] * ext_back[a, first_row : first_row + rows, cols]
        for j in range(1, TAPS):
            start = first_row + j
            acc = acc + taps[a, j : j + 1, cols] * ext_back[a, start : start + rows, cols]
        grads_out[a, first_row : first_row + rows, cols] = acc.astype(BF16)

    @pl.loop(0, 4)
    def _(tile):
        cols = pl.ds(pl.multiple_of(tile * B, B), B)
        for a in range(3):
            for first_row, rows in ((0, 32), (32, 32), (64, 32), (96, 16)):
                reverse(a, first_row, rows, cols)

    @pl.when(me < n - 1)
    def _():
        halo2.wait_recv()
        for a in range(3):
            ext_back[a, B : B + 8, :] = halo2_r[a].astype(F32)

    @pl.loop(0, 4)
    def _(tile):
        cols = pl.ds(pl.multiple_of(tile * B, B), B)
        for a in range(3):
            reverse(a, B - 16, 16, cols)

    @pl.when(me < n - 1)
    def _():
        halo1.wait_send()

    @pl.when(me > 0)
    def _():
        halo2.wait_send()

    all1.wait_send()
    all2.wait_send()


def shards(query_proj, key_proj, value_proj, short_taps, long_filter, grad_mixed):
    rows, channels = query_proj.shape
    filt = long_filter.reshape(PER, B, B).transpose(1, 0, 2).reshape(PER * B, B)
    squares, twist = jnp.asarray(SQUARES), jnp.asarray(TWIST)
    operands = (query_proj, key_proj, value_proj, grad_mixed, short_taps, filt, squares, twist)
    tokens = pltpu.VMEM((rows, channels), BF16)
    edge = pltpu.VMEM((3, 8, channels), BF16)
    blocks = pltpu.VMEM((B, 8, B), BF16)
    tall = pltpu.VMEM((8 * B, B), F32)
    mid = pltpu.VMEM((12 * B, 2 * B), BF16)
    mixed, grads, fgrad = pl.pallas_call(
        kernel,
        name="hyena",
        out_shape=(
            jax.ShapeDtypeStruct((rows, channels), BF16),
            jax.ShapeDtypeStruct((3, rows, channels), BF16),
            jax.ShapeDtypeStruct((PER * B, B), F32),
        ),
        in_specs=[pl.BlockSpec(memory_space=pl.ANY)] * len(operands),
        out_specs=[pl.BlockSpec(memory_space=pltpu.VMEM)] * 3,
        scratch_shapes=[
            tokens, tokens, tokens, tokens,
            pltpu.VMEM(short_taps.shape, F32),
            pltpu.VMEM(filt.shape, F32),
            pltpu.VMEM(squares.shape, BF16),
            pltpu.VMEM(twist.shape, F32),
            pltpu.VMEM((3, rows + 8, channels), F32),
            pltpu.VMEM((3, rows + 8, channels), F32),
            pltpu.VMEM((3, rows, channels), F32),
            edge, edge, edge, edge,
            pltpu.VMEM((rows, 2 * channels), BF16),
            blocks, blocks, blocks, blocks,
            tall, tall,
            mid, mid,
            pltpu.VMEM((12 * B, 2 * B), F32),
            mid, mid,
            pltpu.SemaphoreType.DMA((len(operands),)),
            pltpu.SemaphoreType.DMA((8,)),
        ],
        compiler_params=pltpu.CompilerParams(collective_id=0, has_side_effects=True),
    )(*operands)
    filter_grad = fgrad.reshape(B, PER, B).transpose(1, 0, 2).reshape(1, PER, SEQ)
    return (mixed, grads, filter_grad)


def solution(mesh):
    return jax.shard_map(
        shards,
        mesh=mesh,
        in_specs=(
            P("context", "tensor"),
            P("context", "tensor"),
            P("context", "tensor"),
            P(None, None, "tensor"),
            P("tensor", "context", None),
            P("context", "tensor"),
        ),
        out_specs=(
            P("context", "tensor"),
            P(None, "context", "tensor"),
            P("tensor", "context", None),
        ),
        check_vma=False,
    )
```

```python
import math

import jax
import jax.numpy as jnp
import numpy as np
from jax import lax
from jax.experimental import pallas as pl
from jax.experimental.pallas import tpu as pltpu
from jax.sharding import PartitionSpec as P

MESH = pl.DeviceIdType.MESH
F32 = jnp.float32
BF16 = jnp.bfloat16
B = 128
SEQ = B * B
PER = 4
TAPS = 7
COLS = 16


def split_np(table):
    high = table.astype(jnp.bfloat16)
    low = (table - high.astype(np.float64)).astype(jnp.bfloat16)
    return high, low


def build_tables():
    idx = np.arange(B)
    psi = 2.0 * np.pi * idx[:, None] * (idx[None, :] + 0.25) / B
    phi = 2.0 * np.pi * (idx[:, None] + 0.25) * idx[None, :] / SEQ
    two = 2.0 * np.pi * ((idx[:, None] * idx[None, :]) % B) / B
    first = np.concatenate([np.cos(psi).T, -np.sin(psi).T], axis=0)
    first_back = np.concatenate([np.cos(psi), -np.sin(psi)], axis=1)
    cos, sin = np.cos(two), np.sin(two)
    second = np.block([[cos, -sin], [sin, cos]])
    second_back = np.block([[cos, sin], [-sin, cos]])
    first_cat = np.concatenate(split_np(first), axis=1)
    back_cat = np.concatenate(split_np(first_back), axis=0)
    perm = np.zeros((2 * B, 2 * B))
    for s in range(B // PER):
        for j in range(PER):
            perm[s * 2 * PER + j, PER * s + j] = 1.0
            perm[s * 2 * PER + PER + j, B + PER * s + j] = 1.0
    squares = np.stack(
        [first_cat, *split_np(second), *split_np(second_back), back_cat, perm.astype(jnp.bfloat16)]
    )
    twist = np.stack([np.cos(phi), -np.sin(phi)]).astype(np.float32)
    return squares, twist


SQUARES, TWIST = build_tables()


def split(value):
    high = value.astype(BF16)
    return high, (value - high.astype(F32)).astype(BF16)


def dot(a, b):
    return jnp.dot(a, b, preferred_element_type=F32)


def kernel(
    q_in, k_in, v_in, g_in, taps_in, filt_in, squares_in, twist_in,
    mixed_out, grads_out, fgrad_out,
    q_v, k_v, v_v, g_v, taps, filt, squares, twist,
    ext, ext_back, conv, halo_s, halo_r, halo2_s, halo2_r,
    pair, send1, recv1, send2, recv2, x32, y32,
    mid_hi, mid_lo, spec, prod_hi, prod_lo,
    in_sems, dma_sems, row_sem,
):
    me = lax.axis_index("context")
    n = B

    loads = [
        pltpu.make_async_copy(src, dst, in_sems.at[i])
        for i, (src, dst) in enumerate(
            [
                (q_in, q_v), (k_in, k_v), (v_in, v_v), (taps_in, taps),
                (g_in, g_v), (filt_in, filt), (squares_in, squares), (twist_in, twist),
            ]
        )
    ]
    for load in loads:
        load.start()

    barrier = pltpu.get_barrier_semaphore()
    row, col = me // COLS, lax.rem(me, COLS)

    def signal(sem, peer):
        pl.semaphore_signal(sem, inc=1, device_id={"context": peer}, device_id_type=MESH)

    @pl.when(col == COLS - 1)
    def _():
        signal(barrier, lax.rem(me + 1, n))

    @pl.when(col == 0)
    def _():
        signal(barrier, lax.rem(me + n - 1, n))

    @pl.loop(1, n // COLS)
    def _(i):
        signal(barrier, lax.rem(row + i, n // COLS) * COLS + col)

    @pl.loop(1, COLS)
    def _(i):
        signal(barrier, row * COLS + lax.rem(col + i, COLS))

    def exchange(src, dst, send_sem, recv_sem):
        @pl.loop(1, n)
        def _(i):
            peer = lax.rem(me + i, n)
            pltpu.make_async_remote_copy(
                src_ref=src.at[peer], dst_ref=dst.at[me], send_sem=send_sem, recv_sem=recv_sem,
                device_id={"context": peer}, device_id_type=MESH,
            ).start()

        dst[pl.ds(me, 1)] = src[pl.ds(me, 1)]

    def all_of(src, dst, send_sem, recv_sem):
        return pltpu.make_async_remote_copy(
            src_ref=src.at[pl.ds(0, n - 1)], dst_ref=dst.at[pl.ds(0, n - 1)],
            send_sem=send_sem, recv_sem=recv_sem,
            device_id={"context": lax.rem(me + 1, n)}, device_id_type=MESH,
        )

    def halo_copy(src, dst, send_sem, recv_sem, step):
        return pltpu.make_async_remote_copy(
            src_ref=src, dst_ref=dst, send_sem=send_sem, recv_sem=recv_sem,
            device_id={"context": lax.rem(me + step + n, n)}, device_id_type=MESH,
        )

    for load in loads[:4]:
        load.wait()
    for a, src in enumerate((q_v, k_v, v_v)):
        ext[a, 0:8, :] = jnp.zeros((8, ext.shape[2]), F32)
        halo_s[a] = src[B - 16 : B, :][8:16]

    edge = jnp.logical_or(col == 0, col == COLS - 1)

    @pl.when(edge)
    def _():
        pl.semaphore_wait(barrier, n // COLS + COLS - 1)

    @pl.when(jnp.logical_not(edge))
    def _():
        pl.semaphore_wait(barrier, n // COLS + COLS - 2)

    @pl.loop(1, COLS)
    def _(i):
        signal(row_sem, row * COLS + lax.rem(col + i, COLS))

    halo1 = halo_copy(halo_s, halo_r, dma_sems.at[0], dma_sems.at[1], 1)

    @pl.when(me < n - 1)
    def _():
        halo1.start()

    for load in loads[4:]:
        load.wait()

    def short(a, first_row, rows, cols):
        acc = taps[a, 0:1, cols] * ext[a, 8 + first_row : 8 + first_row + rows, cols]
        for j in range(1, TAPS):
            start = 8 + first_row - j
            acc = acc + taps[a, j : j + 1, cols] * ext[a, start : start + rows, cols]
        return acc

    def gate(first_row, rows, tile):
        cols = pl.ds(pl.multiple_of(tile * B, B), B)
        out = []
        for a in range(3):
            value = short(a, first_row, rows, cols)
            conv[a, first_row : first_row + rows, cols] = value
            out.append(value)
        here = slice(first_row, first_row + rows)
        wide = pl.multiple_of(tile * 2 * B, 2 * B)
        pair[here, pl.ds(wide, B)] = (out[1] * out[2]).astype(BF16)
        pair[here, pl.ds(wide + B, B)] = (g_v[here, cols].astype(F32) * out[0]).astype(BF16)

    @pl.loop(0, 4)
    def _(tile):
        cols = pl.ds(pl.multiple_of(tile * B, B), B)
        for a, src in enumerate((q_v, k_v, v_v)):
            ext[a, 8 : 8 + B, cols] = src[:, cols].astype(F32)
        for first_row in range(0, B, 32):
            gate(first_row, 32, tile)

    @pl.when(me > 0)
    def _():
        halo1.wait_recv()
        for a in range(3):
            ext[a, 0:8, :] = halo_r[a].astype(F32)

    @pl.loop(0, 4)
    def _(tile):
        gate(0, 16, tile)
        wide = pl.multiple_of(tile * 2 * B, 2 * B)
        rows = lax.dot_general(
            squares[6], pair[:, pl.ds(wide, 2 * B)], (((1,), (1,)), ((), ())),
            preferred_element_type=F32,
        )
        send1[pl.ds(pl.multiple_of(tile * 32, 32), 32)] = rows.reshape(32, 8, B).astype(BF16)

    pl.semaphore_wait(row_sem, COLS - 1)
    exchange(send1, recv1, dma_sems.at[2], dma_sems.at[3])
    all1 = all_of(send1, recv1, dma_sems.at[2], dma_sems.at[3])

    tw_re, tw_im = twist[0], twist[1]

    def put_mid(block, stage):
        re, im = stage[:B], stage[B:]
        rows = pl.ds(pl.multiple_of(block * B, B), B)
        for half, value in ((0, re * tw_re - im * tw_im), (1, re * tw_im + im * tw_re)):
            high, low = split(value)
            mid_hi[rows, half * B : half * B + B] = high
            mid_lo[rows, half * B : half * B + B] = low

    def second_stage(chunk):
        rows = pl.ds(pl.multiple_of(chunk * 2 * B, 2 * B), 2 * B)
        high = mid_hi[rows, :]
        spec[rows, :] = dot(high, squares[1]) + dot(mid_lo[rows, :], squares[1]) + dot(high, squares[2])

    @pl.loop(0, PER // 2)
    def _(p):
        rows = [filt[pl.ds(2 * p + i, B, stride=PER), :] for i in range(2)]
        high, low = split(jnp.concatenate(rows, axis=1))
        first = squares[0]
        stage = dot(first, jnp.concatenate([high, high], axis=0)) + dot(first[:, :B], low)
        for i in range(2):
            put_mid(8 + 2 * p + i, stage[:, i * B : i * B + B])
        second_stage(4 + p)

    all1.wait_recv()

    x32[...] = recv1[...].astype(F32).reshape(8 * B, B)

    @pl.loop(0, 4, unroll=4)
    def _(p):
        rows = [x32[pl.ds(2 * p + i, B, stride=8), :].astype(BF16) for i in range(2)]
        signal = jnp.concatenate(rows, axis=1)
        stage = dot(squares[0], jnp.concatenate([signal, signal], axis=0))
        for i in range(2):
            put_mid(2 * p + i, stage[:, i * B : i * B + B])
        second_stage(p)

    def put_prod(block, re, im):
        rows = pl.ds(pl.multiple_of(block * B, B), B)
        for half, value in ((0, re), (1, im)):
            high, low = split(value)
            prod_hi[rows, half * B : half * B + B] = high
            prod_lo[rows, half * B : half * B + B] = low

    def spectrum(block):
        rows = pl.ds(pl.multiple_of(block * B, B), B)
        return spec[rows, 0:B], spec[rows, B : 2 * B]

    @pl.loop(0, PER, unroll=4)
    def _(c):
        x_re, x_im = spectrum(c)
        h_re, h_im = spectrum(8 + c)
        put_prod(c, x_re * h_re - x_im * h_im, x_re * h_im + x_im * h_re)
        g_re, g_im = spectrum(4 + c)
        put_prod(4 + c, h_re * g_re + h_im * g_im, h_re * g_im - h_im * g_re)

    def back(chunk, scale):
        rows = pl.ds(pl.multiple_of(chunk * 2 * B, 2 * B), 2 * B)
        high = prod_hi[rows, :]
        mid = dot(high, squares[3]) + dot(prod_lo[rows, :], squares[3]) + dot(high, squares[4])
        mid = mid * scale
        sides = []
        for i in range(2):
            re, im = mid[i * B : i * B + B, :B], mid[i * B : i * B + B, B:]
            sides.append(
                jnp.concatenate([re * tw_re + im * tw_im, im * tw_re - re * tw_im], axis=0)
            )
        high, low = split(jnp.concatenate(sides, axis=1))
        both = dot(squares[5], high)
        return both[:B] + both[B:] + dot(squares[5, 0:B, :], low)

    @pl.loop(0, 4, unroll=4)
    def _(p):
        result = back(p, 1.0 / SEQ)
        for i in range(2):
            y32[pl.ds(2 * p + i, B, stride=8), :] = result[:, i * B : i * B + B]

    send2[...] = y32[...].reshape(B, 8, B).astype(BF16)
    exchange(send2, recv2, dma_sems.at[4], dma_sems.at[5])

    @pl.loop(0, PER)
    def _(c):
        x_re, x_im = spectrum(c)
        g_re, g_im = spectrum(4 + c)
        put_prod(8 + c, x_re * g_re + x_im * g_im, x_re * g_im - x_im * g_re)

    @pl.loop(0, PER // 2)
    def _(p):
        result = back(4 + p, 1.0 / (SEQ * math.sqrt(SEQ)))
        for i in range(2):
            fgrad_out[pl.ds(2 * p + i, B, stride=PER), :] = result[:, i * B : i * B + B]

    for a in range(3):
        ext_back[a, B : B + 8, :] = jnp.zeros((8, ext_back.shape[2]), F32)
    all2 = all_of(send2, recv2, dma_sems.at[4], dma_sems.at[5])
    all2.wait_recv()

    @pl.loop(0, 4)
    def _(tile):
        cols = pl.ds(pl.multiple_of(tile * B, B), B)
        arrived = recv2[pl.ds(pl.multiple_of(tile * 32, 32), 32)].astype(F32).reshape(2 * B, B)
        rows = dot(arrived.T.astype(BF16), squares[6])
        long, gated_back = rows[:, :B], rows[:, B:]
        mixed_out[:, cols] = (conv[0, :, cols] * long).astype(BF16)
        for a, value in (
            (0, g_v[:, cols].astype(F32) * long),
            (1, gated_back * conv[2, :, cols]),
            (2, gated_back * conv[1, :, cols]),
        ):
            rounded = value.astype(BF16)
            ext_back[a, 0:B, cols] = rounded.astype(F32)
            halo2_s[a, :, cols] = rounded[0:16][0:8]

    halo2 = halo_copy(halo2_s, halo2_r, dma_sems.at[6], dma_sems.at[7], -1)

    @pl.when(me > 0)
    def _():
        halo2.start()

    def reverse(a, first_row, rows, cols):
        acc = taps[a, 0:1, cols] * ext_back[a, first_row : first_row + rows, cols]
        for j in range(1, TAPS):
            start = first_row + j
            acc = acc + taps[a, j : j + 1, cols] * ext_back[a, start : start + rows, cols]
        grads_out[a, first_row : first_row + rows, cols] = acc.astype(BF16)

    @pl.loop(0, 4)
    def _(tile):
        cols = pl.ds(pl.multiple_of(tile * B, B), B)
        for a in range(3):
            for first_row, rows in ((0, 32), (32, 32), (64, 32), (96, 16)):
                reverse(a, first_row, rows, cols)

    @pl.when(me < n - 1)
    def _():
        halo2.wait_recv()
        for a in range(3):
            ext_back[a, B : B + 8, :] = halo2_r[a].astype(F32)

    @pl.loop(0, 4)
    def _(tile):
        cols = pl.ds(pl.multiple_of(tile * B, B), B)
        for a in range(3):
            reverse(a, B - 16, 16, cols)

    @pl.when(me < n - 1)
    def _():
        halo1.wait_send()

    @pl.when(me > 0)
    def _():
        halo2.wait_send()

    all1.wait_send()
    all2.wait_send()


def store(mixed_in, grads_in, fgrad_in, mixed_out, grads_out, fgrad_out, sems):
    copies = [
        pltpu.make_async_copy(src, dst, sems.at[i])
        for i, (src, dst) in enumerate(
            [(grads_in, grads_out), (fgrad_in, fgrad_out), (mixed_in, mixed_out)]
        )
    ]
    for copy in copies:
        copy.start()
    for copy in copies:
        copy.wait()


def shards(query_proj, key_proj, value_proj, short_taps, long_filter, grad_mixed):
    rows, channels = query_proj.shape
    filt = long_filter.reshape(PER, B, B).transpose(1, 0, 2).reshape(PER * B, B)
    squares, twist = jnp.asarray(SQUARES), jnp.asarray(TWIST)
    operands = (query_proj, key_proj, value_proj, grad_mixed, short_taps, filt, squares, twist)
    operands = tuple(pltpu.with_memory_space_constraint(x, pltpu.HBM) for x in operands)
    tokens = pltpu.VMEM((rows, channels), BF16)
    edge = pltpu.VMEM((3, 8, channels), BF16)
    blocks = pltpu.VMEM((B, 8, B), BF16)
    tall = pltpu.VMEM((8 * B, B), F32)
    mid = pltpu.VMEM((12 * B, 2 * B), BF16)
    out_shape = (
        jax.ShapeDtypeStruct((rows, channels), BF16),
        jax.ShapeDtypeStruct((3, rows, channels), BF16),
        jax.ShapeDtypeStruct((PER * B, B), F32),
    )
    results = pl.pallas_call(
        kernel,
        name="hyena",
        out_shape=out_shape,
        in_specs=[pl.BlockSpec(memory_space=pl.ANY)] * len(operands),
        out_specs=[pl.BlockSpec(memory_space=pltpu.VMEM)] * 3,
        scratch_shapes=[
            tokens, tokens, tokens, tokens,
            pltpu.VMEM(short_taps.shape, F32),
            pltpu.VMEM(filt.shape, F32),
            pltpu.VMEM(squares.shape, BF16),
            pltpu.VMEM(twist.shape, F32),
            pltpu.VMEM((3, rows + 8, channels), F32),
            pltpu.VMEM((3, rows + 8, channels), F32),
            pltpu.VMEM((3, rows, channels), F32),
            edge, edge, edge, edge,
            pltpu.VMEM((rows, 2 * channels), BF16),
            blocks, blocks, blocks, blocks,
            tall, tall,
            mid, mid,
            pltpu.VMEM((12 * B, 2 * B), F32),
            mid, mid,
            pltpu.SemaphoreType.DMA((len(operands),)),
            pltpu.SemaphoreType.DMA((8,)),
            pltpu.SemaphoreType.REGULAR,
        ],
        compiler_params=pltpu.CompilerParams(collective_id=0, has_side_effects=True, vmem_limit_bytes=24 * 1024 * 1024),
    )(*operands)
    mixed, grads, fgrad = pl.pallas_call(
        store,
        name="store",
        out_shape=out_shape,
        in_specs=[pl.BlockSpec(memory_space=pltpu.VMEM)] * 3,
        out_specs=[pl.BlockSpec(memory_space=pl.ANY)] * 3,
        scratch_shapes=[pltpu.SemaphoreType.DMA((3,))],
        compiler_params=pltpu.CompilerParams(vmem_limit_bytes=2 * 1024 * 1024),
    )(*results)
    filter_grad = fgrad.reshape(B, PER, B).transpose(1, 0, 2).reshape(1, PER, SEQ)
    return (mixed, grads, filter_grad)


def solution(mesh):
    return jax.shard_map(
        shards,
        mesh=mesh,
        in_specs=(
            P("context", "tensor"),
            P("context", "tensor"),
            P("context", "tensor"),
            P(None, None, "tensor"),
            P("tensor", "context", None),
            P("context", "tensor"),
        ),
        out_specs=(
            P("context", "tensor"),
            P(None, "context", "tensor"),
            P("tensor", "context", None),
        ),
        check_vma=False,
    )
```

```python
import math

import jax
import jax.numpy as jnp
import numpy as np
from jax import lax
from jax.experimental import pallas as pl
from jax.experimental.pallas import tpu as pltpu
from jax.sharding import PartitionSpec as P

MESH = pl.DeviceIdType.MESH
F32 = jnp.float32
BF16 = jnp.bfloat16
B = 128
SEQ = B * B
PER = 4
TAPS = 7
COLS = 16


def split_np(table):
    high = table.astype(jnp.bfloat16)
    low = (table - high.astype(np.float64)).astype(jnp.bfloat16)
    return high, low


def build_tables():
    idx = np.arange(B)
    psi = 2.0 * np.pi * idx[:, None] * (idx[None, :] + 0.25) / B
    phi = 2.0 * np.pi * (idx[:, None] + 0.25) * idx[None, :] / SEQ
    two = 2.0 * np.pi * ((idx[:, None] * idx[None, :]) % B) / B
    first = np.concatenate([np.cos(psi).T, -np.sin(psi).T], axis=0)
    first_back = np.concatenate([np.cos(psi), -np.sin(psi)], axis=1)
    cos, sin = np.cos(two), np.sin(two)
    second = np.block([[cos, -sin], [sin, cos]])
    second_back = np.block([[cos, sin], [-sin, cos]])
    first_cat = np.concatenate(split_np(first), axis=1)
    back_cat = np.concatenate(split_np(first_back), axis=0)
    perm = np.zeros((2 * B, 2 * B))
    for s in range(B // PER):
        for j in range(PER):
            perm[s * 2 * PER + j, PER * s + j] = 1.0
            perm[s * 2 * PER + PER + j, B + PER * s + j] = 1.0
    squares = np.stack(
        [first_cat, *split_np(second), *split_np(second_back), back_cat, perm.astype(jnp.bfloat16)]
    )
    twist = np.stack([np.cos(phi), -np.sin(phi), np.cos(phi) / SEQ, np.sin(phi) / SEQ])
    twist = twist.astype(np.float32)
    return squares, twist


SQUARES, TWIST = build_tables()


def split(value):
    high = value.astype(BF16)
    return high, (value - high.astype(F32)).astype(BF16)


def dot(a, b):
    return jnp.dot(a, b, preferred_element_type=F32)


def kernel(
    q_in, k_in, v_in, g_in, taps_in, filt_in, squares_in, twist_in,
    mixed_out, grads_out, fgrad_out,
    q_v, k_v, v_v, g_v, taps, filt, squares, twist,
    ext, ext_back, conv, halo_s, halo_r, halo2_s, halo2_r,
    pair, send1, recv1, send2, recv2, x32, y32,
    mid_hi, mid_lo, spec, prod_hi, prod_lo,
    in_sems, dma_sems, row_sem,
):
    me = lax.axis_index("context")
    n = B

    loads = [
        pltpu.make_async_copy(src, dst, in_sems.at[i])
        for i, (src, dst) in enumerate(
            [
                (q_in, q_v), (k_in, k_v), (v_in, v_v), (taps_in, taps),
                (g_in, g_v), (filt_in, filt), (squares_in, squares), (twist_in, twist),
            ]
        )
    ]
    for load in loads:
        load.start()

    barrier = pltpu.get_barrier_semaphore()
    row, col = me // COLS, lax.rem(me, COLS)

    def signal(sem, peer):
        pl.semaphore_signal(sem, inc=1, device_id={"context": peer}, device_id_type=MESH)

    @pl.when(col == COLS - 1)
    def _():
        signal(barrier, lax.rem(me + 1, n))

    @pl.when(col == 0)
    def _():
        signal(barrier, lax.rem(me + n - 1, n))

    @pl.loop(1, n // COLS)
    def _(i):
        signal(barrier, lax.rem(row + i, n // COLS) * COLS + col)

    @pl.loop(1, COLS)
    def _(i):
        signal(barrier, row * COLS + lax.rem(col + i, COLS))

    def sender(src, dst, send_sem, recv_sem):
        def send(peer):
            pltpu.make_async_remote_copy(
                src_ref=src.at[peer], dst_ref=dst.at[me], send_sem=send_sem, recv_sem=recv_sem,
                device_id={"context": peer}, device_id_type=MESH,
            ).start()

        return send

    def all_of(src, dst, send_sem, recv_sem):
        return pltpu.make_async_remote_copy(
            src_ref=src.at[pl.ds(0, n - 1)], dst_ref=dst.at[pl.ds(0, n - 1)],
            send_sem=send_sem, recv_sem=recv_sem,
            device_id={"context": lax.rem(me + 1, n)}, device_id_type=MESH,
        )

    def halo_copy(src, dst, send_sem, recv_sem, step):
        return pltpu.make_async_remote_copy(
            src_ref=src, dst_ref=dst, send_sem=send_sem, recv_sem=recv_sem,
            device_id={"context": lax.rem(me + step + n, n)}, device_id_type=MESH,
        )

    for load in loads[:4]:
        load.wait()
    for a, src in enumerate((q_v, k_v, v_v)):
        ext[a, 0:8, :] = jnp.zeros((8, ext.shape[2]), F32)
        halo_s[a] = src[B - 16 : B, :][8:16]

    edge = jnp.logical_or(col == 0, col == COLS - 1)

    @pl.when(edge)
    def _():
        pl.semaphore_wait(barrier, n // COLS + COLS - 1)

    @pl.when(jnp.logical_not(edge))
    def _():
        pl.semaphore_wait(barrier, n // COLS + COLS - 2)

    @pl.loop(1, COLS)
    def _(i):
        signal(row_sem, row * COLS + lax.rem(col + i, COLS))

    halo1 = halo_copy(halo_s, halo_r, dma_sems.at[0], dma_sems.at[1], 1)

    @pl.when(me < n - 1)
    def _():
        halo1.start()

    for load in loads[4:]:
        load.wait()

    def short(a, first_row, rows, cols):
        acc = taps[a, 0:1, cols] * ext[a, 8 + first_row : 8 + first_row + rows, cols]
        for j in range(1, TAPS):
            start = 8 + first_row - j
            acc = acc + taps[a, j : j + 1, cols] * ext[a, start : start + rows, cols]
        return acc

    def gate(first_row, rows, tile):
        cols = pl.ds(pl.multiple_of(tile * B, B), B)
        out = []
        for a in range(3):
            value = short(a, first_row, rows, cols)
            conv[a, first_row : first_row + rows, cols] = value
            out.append(value)
        here = slice(first_row, first_row + rows)
        wide = pl.multiple_of(tile * 2 * B, 2 * B)
        pair[here, pl.ds(wide, B)] = (out[1] * out[2]).astype(BF16)
        pair[here, pl.ds(wide + B, B)] = (g_v[here, cols].astype(F32) * out[0]).astype(BF16)

    @pl.loop(0, 4)
    def _(tile):
        cols = pl.ds(pl.multiple_of(tile * B, B), B)
        for a, src in enumerate((q_v, k_v, v_v)):
            ext[a, 8 : 8 + B, cols] = src[:, cols].astype(F32)
        for first_row in range(0, B, 32):
            gate(first_row, 32, tile)

    @pl.when(me > 0)
    def _():
        halo1.wait_recv()
        for a in range(3):
            ext[a, 0:8, :] = halo_r[a].astype(F32)

    @pl.loop(0, 4)
    def _(tile):
        gate(0, 16, tile)
        wide = pl.multiple_of(tile * 2 * B, 2 * B)
        rows = lax.dot_general(
            squares[6], pair[:, pl.ds(wide, 2 * B)], (((1,), (1,)), ((), ())),
            preferred_element_type=F32,
        )
        send1[pl.ds(pl.multiple_of(tile * 32, 32), 32)] = rows.reshape(32, 8, B).astype(BF16)

    send = sender(send1, recv1, dma_sems.at[2], dma_sems.at[3])
    for i in range(1, n // COLS):
        send(lax.rem(row + i, n // COLS) * COLS + col)

    @pl.loop(0, (COLS - 1) // 3)
    def _(i):
        for u in range(3):
            send(row * COLS + lax.rem(col + 3 * i + 1 + u, COLS))

    pl.semaphore_wait(row_sem, COLS - 1)

    @pl.loop(1, n // COLS)
    def _(i):
        start = lax.rem(row + i, n // COLS) * COLS
        for u in range(1, COLS):
            send(start + lax.rem(col + u, COLS))

    recv1[pl.ds(me, 1)] = send1[pl.ds(me, 1)]
    all1 = all_of(send1, recv1, dma_sems.at[2], dma_sems.at[3])

    tw_re, tw_im = twist[0], twist[1]
    back_re, back_im = twist[2], twist[3]

    def put_mid(block, stage):
        re, im = stage[:B], stage[B:]
        rows = pl.ds(pl.multiple_of(block * B, B), B)
        for half, value in ((0, re * tw_re - im * tw_im), (1, re * tw_im + im * tw_re)):
            high, low = split(value)
            mid_hi[rows, half * B : half * B + B] = high
            mid_lo[rows, half * B : half * B + B] = low

    def second_stage(rows):
        high = mid_hi[rows, :]
        spec[rows, :] = dot(high, squares[1]) + dot(mid_lo[rows, :], squares[1]) + dot(high, squares[2])

    @pl.loop(0, PER // 2)
    def _(p):
        rows = [filt[pl.ds(2 * p + i, B, stride=PER), :] for i in range(2)]
        high, low = split(jnp.concatenate(rows, axis=1))
        first = squares[0]
        stage = dot(first, jnp.concatenate([high, high], axis=0)) + dot(first[:, :B], low)
        for i in range(2):
            put_mid(8 + 2 * p + i, stage[:, i * B : i * B + B])
        second_stage(pl.ds(pl.multiple_of((4 + p) * 2 * B, 2 * B), 2 * B))

    all1.wait_recv()

    x32[...] = recv1[...].astype(F32).reshape(8 * B, B)

    @pl.loop(0, 4, unroll=4)
    def _(p):
        rows = [x32[pl.ds(2 * p + i, B, stride=8), :].astype(BF16) for i in range(2)]
        signal = jnp.concatenate(rows, axis=1)
        stage = dot(squares[0], jnp.concatenate([signal, signal], axis=0))
        for i in range(2):
            put_mid(2 * p + i, stage[:, i * B : i * B + B])

    second_stage(slice(0, 8 * B))

    def put_prod(block, re, im):
        rows = pl.ds(pl.multiple_of(block * B, B), B)
        for half, value in ((0, re), (1, im)):
            high, low = split(value)
            prod_hi[rows, half * B : half * B + B] = high
            prod_lo[rows, half * B : half * B + B] = low

    def spectrum(block):
        rows = pl.ds(pl.multiple_of(block * B, B), B)
        return spec[rows, 0:B], spec[rows, B : 2 * B]

    @pl.loop(0, PER, unroll=4)
    def _(c):
        x_re, x_im = spectrum(c)
        h_re, h_im = spectrum(8 + c)
        put_prod(c, x_re * h_re - x_im * h_im, x_re * h_im + x_im * h_re)
        g_re, g_im = spectrum(4 + c)
        put_prod(4 + c, h_re * g_re + h_im * g_im, h_re * g_im - h_im * g_re)

    def second_back(rows):
        high = prod_hi[rows, :]
        return dot(high, squares[3]) + dot(prod_lo[rows, :], squares[3]) + dot(high, squares[4])

    def first_back(mid):
        sides = []
        for i in range(2):
            re, im = mid[i * B : i * B + B, :B], mid[i * B : i * B + B, B:]
            sides.append(
                jnp.concatenate([re * back_re - im * back_im, im * back_re + re * back_im], axis=0)
            )
        high, low = split(jnp.concatenate(sides, axis=1))
        both = dot(squares[5], high)
        return both[:B] + both[B:] + dot(squares[5, 0:B, :], low)

    mids = second_back(slice(0, 8 * B))
    for p in range(4):
        result = first_back(mids[2 * B * p : 2 * B * (p + 1)])
        for i in range(2):
            y32[pl.ds(2 * p + i, B, stride=8), :] = result[:, i * B : i * B + B]

    send2[...] = y32[...].reshape(B, 8, B).astype(BF16)
    send = sender(send2, recv2, dma_sems.at[4], dma_sems.at[5])

    @pl.loop(0, (n - 2) // 3)
    def _(i):
        for u in range(3):
            send(lax.rem(me + 3 * i + 1 + u, n))

    send(lax.rem(me + n - 1, n))
    recv2[pl.ds(me, 1)] = send2[pl.ds(me, 1)]

    @pl.loop(0, PER)
    def _(c):
        x_re, x_im = spectrum(c)
        g_re, g_im = spectrum(4 + c)
        put_prod(8 + c, x_re * g_re + x_im * g_im, x_re * g_im - x_im * g_re)

    @pl.loop(0, PER // 2)
    def _(p):
        mid = second_back(pl.ds(pl.multiple_of((4 + p) * 2 * B, 2 * B), 2 * B))
        result = first_back(mid) * (1.0 / math.sqrt(SEQ))
        for i in range(2):
            fgrad_out[pl.ds(2 * p + i, B, stride=PER), :] = result[:, i * B : i * B + B]

    for a in range(3):
        ext_back[a, B : B + 8, :] = jnp.zeros((8, ext_back.shape[2]), F32)
    all2 = all_of(send2, recv2, dma_sems.at[4], dma_sems.at[5])
    all2.wait_recv()

    def gradients(here, cols, long, gated_back):
        return (
            (g_v[here, cols].astype(F32) * long).astype(BF16),
            (gated_back * conv[2, here, cols]).astype(BF16),
            (gated_back * conv[1, here, cols]).astype(BF16),
        )

    eye = jnp.where(
        lax.broadcasted_iota(jnp.int32, (16, B), 0) == lax.broadcasted_iota(jnp.int32, (16, B), 1),
        1.0, 0.0,
    ).astype(BF16)
    for tile in range(4):
        cols = slice(tile * B, tile * B + B)
        arrived = recv2[tile * 32 : tile * 32 + 32].astype(F32).reshape(2 * B, B).astype(BF16)
        head = lax.dot_general(
            eye, arrived, (((1,), (1,)), ((), ())), preferred_element_type=F32
        ).astype(BF16)
        head = dot(head, squares[6])
        for a, value in enumerate(gradients(slice(0, 16), cols, head[:, :B], head[:, B:])):
            halo2_s[a, :, cols] = value[0:8]

    halo2 = halo_copy(halo2_s, halo2_r, dma_sems.at[6], dma_sems.at[7], -1)

    @pl.when(me > 0)
    def _():
        halo2.start()

    @pl.loop(0, 4, unroll=2)
    def _(tile):
        cols = pl.ds(pl.multiple_of(tile * B, B), B)
        arrived = recv2[pl.ds(pl.multiple_of(tile * 32, 32), 32)].astype(F32).reshape(2 * B, B)
        rows = dot(arrived.T.astype(BF16), squares[6])
        long, gated_back = rows[:, :B], rows[:, B:]
        mixed_out[:, cols] = (conv[0, :, cols] * long).astype(BF16)
        for a, value in enumerate(gradients(slice(0, B), cols, long, gated_back)):
            ext_back[a, 0:B, cols] = value.astype(F32)

    def reverse(a, first_row, rows, cols):
        acc = taps[a, 0:1, cols] * ext_back[a, first_row : first_row + rows, cols]
        for j in range(1, TAPS):
            start = first_row + j
            acc = acc + taps[a, j : j + 1, cols] * ext_back[a, start : start + rows, cols]
        grads_out[a, first_row : first_row + rows, cols] = acc.astype(BF16)

    @pl.loop(0, 4)
    def _(tile):
        cols = pl.ds(pl.multiple_of(tile * B, B), B)
        for a in range(3):
            for first_row, rows in ((0, 32), (32, 32), (64, 32), (96, 16)):
                reverse(a, first_row, rows, cols)

    @pl.when(me < n - 1)
    def _():
        halo2.wait_recv()
        for a in range(3):
            ext_back[a, B : B + 8, :] = halo2_r[a].astype(F32)

    @pl.loop(0, 4, unroll=True)
    def _(tile):
        cols = pl.ds(pl.multiple_of(tile * B, B), B)
        for a in range(3):
            reverse(a, B - 16, 16, cols)

    @pl.when(me < n - 1)
    def _():
        halo1.wait_send()

    @pl.when(me > 0)
    def _():
        halo2.wait_send()

    all1.wait_send()
    all2.wait_send()


def store(mixed_in, grads_in, fgrad_in, mixed_out, grads_out, fgrad_out, sems):
    copies = [
        pltpu.make_async_copy(src, dst, sems.at[i])
        for i, (src, dst) in enumerate(
            [(grads_in, grads_out), (fgrad_in, fgrad_out), (mixed_in, mixed_out)]
        )
    ]
    for copy in copies:
        copy.start()
    for copy in copies:
        copy.wait()


def shards(query_proj, key_proj, value_proj, short_taps, long_filter, grad_mixed):
    rows, channels = query_proj.shape
    filt = long_filter.reshape(PER, B, B).transpose(1, 0, 2).reshape(PER * B, B)
    squares, twist = jnp.asarray(SQUARES), jnp.asarray(TWIST)
    operands = (query_proj, key_proj, value_proj, grad_mixed, short_taps, filt, squares, twist)
    operands = tuple(pltpu.with_memory_space_constraint(x, pltpu.HBM) for x in operands)
    tokens = pltpu.VMEM((rows, channels), BF16)
    edge = pltpu.VMEM((3, 8, channels), BF16)
    blocks = pltpu.VMEM((B, 8, B), BF16)
    tall = pltpu.VMEM((8 * B, B), F32)
    mid = pltpu.VMEM((12 * B, 2 * B), BF16)
    out_shape = (
        jax.ShapeDtypeStruct((rows, channels), BF16),
        jax.ShapeDtypeStruct((3, rows, channels), BF16),
        jax.ShapeDtypeStruct((PER * B, B), F32),
    )
    results = pl.pallas_call(
        kernel,
        name="hyena",
        out_shape=out_shape,
        in_specs=[pl.BlockSpec(memory_space=pl.ANY)] * len(operands),
        out_specs=[pl.BlockSpec(memory_space=pltpu.VMEM)] * 3,
        scratch_shapes=[
            tokens, tokens, tokens, tokens,
            pltpu.VMEM(short_taps.shape, F32),
            pltpu.VMEM(filt.shape, F32),
            pltpu.VMEM(squares.shape, BF16),
            pltpu.VMEM(twist.shape, F32),
            pltpu.VMEM((3, rows + 8, channels), F32),
            pltpu.VMEM((3, rows + 8, channels), F32),
            pltpu.VMEM((3, rows, channels), F32),
            edge, edge, edge, edge,
            pltpu.VMEM((rows, 2 * channels), BF16),
            blocks, blocks, blocks, blocks,
            tall, tall,
            mid, mid,
            pltpu.VMEM((12 * B, 2 * B), F32),
            mid, mid,
            pltpu.SemaphoreType.DMA((len(operands),)),
            pltpu.SemaphoreType.DMA((8,)),
            pltpu.SemaphoreType.REGULAR,
        ],
        compiler_params=pltpu.CompilerParams(collective_id=0, has_side_effects=True, vmem_limit_bytes=24 * 1024 * 1024),
    )(*operands)
    mixed, grads, fgrad = pl.pallas_call(
        store,
        name="store",
        out_shape=out_shape,
        in_specs=[pl.BlockSpec(memory_space=pltpu.VMEM)] * 3,
        out_specs=[pl.BlockSpec(memory_space=pl.ANY)] * 3,
        scratch_shapes=[pltpu.SemaphoreType.DMA((3,))],
        compiler_params=pltpu.CompilerParams(vmem_limit_bytes=2 * 1024 * 1024),
    )(*results)
    filter_grad = fgrad.reshape(B, PER, B).transpose(1, 0, 2).reshape(1, PER, SEQ)
    return (mixed, grads, filter_grad)


def solution(mesh):
    return jax.shard_map(
        shards,
        mesh=mesh,
        in_specs=(
            P("context", "tensor"),
            P("context", "tensor"),
            P("context", "tensor"),
            P(None, None, "tensor"),
            P("tensor", "context", None),
            P("context", "tensor"),
        ),
        out_specs=(
            P("context", "tensor"),
            P(None, "context", "tensor"),
            P("tensor", "context", None),
        ),
        check_vma=False,
    )
```

```python
import math

import jax
import jax.numpy as jnp
import numpy as np
from jax import lax
from jax.experimental import pallas as pl
from jax.experimental.pallas import tpu as pltpu
from jax.sharding import PartitionSpec as P

MESH = pl.DeviceIdType.MESH
F32 = jnp.float32
BF16 = jnp.bfloat16
B = 128
SEQ = B * B
PER = 4
TAPS = 7
COLS = 16


def split_np(table):
    high = table.astype(jnp.bfloat16)
    low = (table - high.astype(np.float64)).astype(jnp.bfloat16)
    return high, low


def build_tables():
    idx = np.arange(B)
    psi = 2.0 * np.pi * idx[:, None] * (idx[None, :] + 0.25) / B
    phi = 2.0 * np.pi * (idx[:, None] + 0.25) * idx[None, :] / SEQ
    two = 2.0 * np.pi * ((idx[:, None] * idx[None, :]) % B) / B
    first = np.concatenate([np.cos(psi).T, -np.sin(psi).T], axis=0)
    first_back = np.concatenate([np.cos(psi), -np.sin(psi)], axis=1)
    cos, sin = np.cos(two), np.sin(two)
    second = np.block([[cos, -sin], [sin, cos]])
    second_back = np.block([[cos, sin], [-sin, cos]])
    first_cat = np.concatenate(split_np(first), axis=1)
    back_cat = np.concatenate(split_np(first_back), axis=0)
    perm = np.zeros((2 * B, 2 * B))
    for s in range(B // PER):
        for j in range(PER):
            perm[s * 2 * PER + j, PER * s + j] = 1.0
            perm[s * 2 * PER + PER + j, B + PER * s + j] = 1.0
    squares = np.stack(
        [first_cat, *split_np(second), *split_np(second_back), back_cat, perm.astype(jnp.bfloat16)]
    )
    twist = np.stack([np.cos(phi), -np.sin(phi), np.cos(phi) / SEQ, np.sin(phi) / SEQ])
    twist = twist.astype(np.float32)
    return squares, twist


SQUARES, TWIST = build_tables()


def split(value):
    high = value.astype(BF16)
    return high, (value - high.astype(F32)).astype(BF16)


def dot(a, b):
    return jnp.dot(a, b, preferred_element_type=F32)


def kernel(
    q_in, k_in, v_in, g_in, taps_in, filt_in, squares_in, twist_in,
    mixed_out, grads_out, fgrad_out,
    q_v, k_v, v_v, g_v, taps, filt, squares, twist,
    ext, ext_back, conv, halo_s, halo_r, halo2_s, halo2_r,
    pair, send1, recv1, send2, recv2, x32, y32,
    mid_hi, mid_lo, spec, prod_hi, prod_lo,
    in_sems, dma_sems, row_sem,
):
    me = lax.axis_index("context")
    n = B

    loads = [
        pltpu.make_async_copy(src, dst, in_sems.at[i])
        for i, (src, dst) in enumerate(
            [
                (q_in, q_v), (k_in, k_v), (v_in, v_v), (taps_in, taps),
                (g_in, g_v), (filt_in, filt), (squares_in, squares), (twist_in, twist),
            ]
        )
    ]
    for load in loads:
        load.start()

    barrier = pltpu.get_barrier_semaphore()
    row, col = me // COLS, lax.rem(me, COLS)

    def signal(sem, peer):
        pl.semaphore_signal(sem, inc=1, device_id={"context": peer}, device_id_type=MESH)

    @pl.when(col == COLS - 1)
    def _():
        signal(barrier, lax.rem(me + 1, n))

    @pl.when(col == 0)
    def _():
        signal(barrier, lax.rem(me + n - 1, n))

    @pl.loop(1, n // COLS)
    def _(i):
        signal(barrier, lax.rem(row + i, n // COLS) * COLS + col)

    @pl.loop(1, COLS)
    def _(i):
        signal(barrier, row * COLS + lax.rem(col + i, COLS))

    def sender(src, dst, send_sem, recv_sem):
        def send(peer):
            pltpu.make_async_remote_copy(
                src_ref=src.at[peer], dst_ref=dst.at[me], send_sem=send_sem, recv_sem=recv_sem,
                device_id={"context": peer}, device_id_type=MESH,
            ).start()

        return send

    def all_of(src, dst, send_sem, recv_sem):
        return pltpu.make_async_remote_copy(
            src_ref=src.at[pl.ds(0, n - 1)], dst_ref=dst.at[pl.ds(0, n - 1)],
            send_sem=send_sem, recv_sem=recv_sem,
            device_id={"context": lax.rem(me + 1, n)}, device_id_type=MESH,
        )

    def halo_copy(src, dst, send_sem, recv_sem, step):
        return pltpu.make_async_remote_copy(
            src_ref=src, dst_ref=dst, send_sem=send_sem, recv_sem=recv_sem,
            device_id={"context": lax.rem(me + step + n, n)}, device_id_type=MESH,
        )

    for load in loads[:4]:
        load.wait()
    for a, src in enumerate((q_v, k_v, v_v)):
        ext[a, 0:8, :] = jnp.zeros((8, ext.shape[2]), F32)
        halo_s[a] = src[B - 16 : B, :][8:16]

    edge = jnp.logical_or(col == 0, col == COLS - 1)

    @pl.when(edge)
    def _():
        pl.semaphore_wait(barrier, n // COLS + COLS - 1)

    @pl.when(jnp.logical_not(edge))
    def _():
        pl.semaphore_wait(barrier, n // COLS + COLS - 2)

    @pl.loop(1, COLS)
    def _(i):
        signal(row_sem, row * COLS + lax.rem(col + i, COLS))

    halo1 = halo_copy(halo_s, halo_r, dma_sems.at[0], dma_sems.at[1], 1)

    @pl.when(me < n - 1)
    def _():
        halo1.start()

    for load in loads[4:]:
        load.wait()

    def short(a, first_row, rows, cols):
        acc = taps[a, 0:1, cols] * ext[a, 8 + first_row : 8 + first_row + rows, cols]
        for j in range(1, TAPS):
            start = 8 + first_row - j
            acc = acc + taps[a, j : j + 1, cols] * ext[a, start : start + rows, cols]
        return acc

    def gate(first_row, rows, tile):
        cols = pl.ds(pl.multiple_of(tile * B, B), B)
        out = []
        for a in range(3):
            value = short(a, first_row, rows, cols)
            conv[a, first_row : first_row + rows, cols] = value
            out.append(value)
        here = slice(first_row, first_row + rows)
        wide = pl.multiple_of(tile * 2 * B, 2 * B)
        pair[here, pl.ds(wide, B)] = (out[1] * out[2]).astype(BF16)
        pair[here, pl.ds(wide + B, B)] = (g_v[here, cols].astype(F32) * out[0]).astype(BF16)

    @pl.loop(0, 4)
    def _(tile):
        cols = pl.ds(pl.multiple_of(tile * B, B), B)
        for a, src in enumerate((q_v, k_v, v_v)):
            ext[a, 8 : 8 + B, cols] = src[:, cols].astype(F32)
        for first_row in range(0, B, 32):
            gate(first_row, 32, tile)

    @pl.when(me > 0)
    def _():
        halo1.wait_recv()
        for a in range(3):
            ext[a, 0:8, :] = halo_r[a].astype(F32)

    @pl.loop(0, 4, unroll=True)
    def _(tile):
        gate(0, 16, tile)
        wide = pl.multiple_of(tile * 2 * B, 2 * B)
        rows = lax.dot_general(
            squares[6], pair[:, pl.ds(wide, 2 * B)], (((1,), (1,)), ((), ())),
            preferred_element_type=F32,
        )
        send1[pl.ds(pl.multiple_of(tile * 32, 32), 32)] = rows.reshape(32, 8, B).astype(BF16)

    send = sender(send1, recv1, dma_sems.at[2], dma_sems.at[3])
    for i in range(1, n // COLS):
        send(lax.rem(row + i, n // COLS) * COLS + col)

    @pl.loop(0, (COLS - 1) // 3)
    def _(i):
        for u in range(3):
            send(row * COLS + lax.rem(col + 3 * i + 1 + u, COLS))

    pl.semaphore_wait(row_sem, COLS - 1)

    @pl.loop(1, n // COLS)
    def _(i):
        start = lax.rem(row + i, n // COLS) * COLS
        for u in range(1, COLS):
            send(start + lax.rem(col + u, COLS))

    recv1[pl.ds(me, 1)] = send1[pl.ds(me, 1)]
    all1 = all_of(send1, recv1, dma_sems.at[2], dma_sems.at[3])

    tw_re, tw_im = twist[0], twist[1]
    back_re, back_im = twist[2], twist[3]

    def put_mid(block, stage):
        re, im = stage[:B], stage[B:]
        rows = pl.ds(pl.multiple_of(block * B, B), B)
        for half, value in ((0, re * tw_re - im * tw_im), (1, re * tw_im + im * tw_re)):
            high, low = split(value)
            mid_hi[rows, half * B : half * B + B] = high
            mid_lo[rows, half * B : half * B + B] = low

    def second_stage(rows):
        high = mid_hi[rows, :]
        spec[rows, :] = dot(high, squares[1]) + dot(mid_lo[rows, :], squares[1]) + dot(high, squares[2])

    @pl.loop(0, PER // 2)
    def _(p):
        rows = [filt[pl.ds(2 * p + i, B, stride=PER), :] for i in range(2)]
        high, low = split(jnp.concatenate(rows, axis=1))
        first = squares[0]
        stage = dot(first, jnp.concatenate([high, high], axis=0)) + dot(first[:, :B], low)
        for i in range(2):
            put_mid(8 + 2 * p + i, stage[:, i * B : i * B + B])
        second_stage(pl.ds(pl.multiple_of((4 + p) * 2 * B, 2 * B), 2 * B))

    all1.wait_recv()

    x32[...] = recv1[...].astype(F32).reshape(8 * B, B)

    @pl.loop(0, 4, unroll=4)
    def _(p):
        rows = [x32[pl.ds(2 * p + i, B, stride=8), :].astype(BF16) for i in range(2)]
        signal = jnp.concatenate(rows, axis=1)
        stage = dot(squares[0], jnp.concatenate([signal, signal], axis=0))
        for i in range(2):
            put_mid(2 * p + i, stage[:, i * B : i * B + B])

    second_stage(slice(0, 8 * B))

    def put_prod(block, re, im):
        rows = pl.ds(pl.multiple_of(block * B, B), B)
        for half, value in ((0, re), (1, im)):
            high, low = split(value)
            prod_hi[rows, half * B : half * B + B] = high
            prod_lo[rows, half * B : half * B + B] = low

    def spectrum(block):
        rows = pl.ds(pl.multiple_of(block * B, B), B)
        return spec[rows, 0:B], spec[rows, B : 2 * B]

    @pl.loop(0, PER, unroll=4)
    def _(c):
        x_re, x_im = spectrum(c)
        h_re, h_im = spectrum(8 + c)
        put_prod(c, x_re * h_re - x_im * h_im, x_re * h_im + x_im * h_re)
        g_re, g_im = spectrum(4 + c)
        put_prod(4 + c, h_re * g_re + h_im * g_im, h_re * g_im - h_im * g_re)

    def second_back(rows):
        high = prod_hi[rows, :]
        return dot(high, squares[3]) + dot(prod_lo[rows, :], squares[3]) + dot(high, squares[4])

    def first_back(mid):
        sides = []
        for i in range(2):
            re, im = mid[i * B : i * B + B, :B], mid[i * B : i * B + B, B:]
            sides.append(
                jnp.concatenate([re * back_re - im * back_im, im * back_re + re * back_im], axis=0)
            )
        high, low = split(jnp.concatenate(sides, axis=1))
        both = dot(squares[5], high)
        return both[:B] + both[B:] + dot(squares[5, 0:B, :], low)

    mids = second_back(slice(0, 8 * B))
    for p in range(4):
        result = first_back(mids[2 * B * p : 2 * B * (p + 1)])
        for i in range(2):
            y32[pl.ds(2 * p + i, B, stride=8), :] = result[:, i * B : i * B + B]

    send2[...] = y32[...].reshape(B, 8, B).astype(BF16)
    send = sender(send2, recv2, dma_sems.at[4], dma_sems.at[5])

    @pl.loop(0, (n - 2) // 3)
    def _(i):
        for u in range(3):
            send(lax.rem(me + 3 * i + 1 + u, n))

    send(lax.rem(me + n - 1, n))
    recv2[pl.ds(me, 1)] = send2[pl.ds(me, 1)]

    @pl.loop(0, PER)
    def _(c):
        x_re, x_im = spectrum(c)
        g_re, g_im = spectrum(4 + c)
        put_prod(8 + c, x_re * g_re + x_im * g_im, x_re * g_im - x_im * g_re)

    @pl.loop(0, PER // 2)
    def _(p):
        mid = second_back(pl.ds(pl.multiple_of((4 + p) * 2 * B, 2 * B), 2 * B))
        result = first_back(mid) * (1.0 / math.sqrt(SEQ))
        for i in range(2):
            fgrad_out[pl.ds(2 * p + i, B, stride=PER), :] = result[:, i * B : i * B + B]

    for a in range(3):
        ext_back[a, B : B + 8, :] = jnp.zeros((8, ext_back.shape[2]), F32)
    all2 = all_of(send2, recv2, dma_sems.at[4], dma_sems.at[5])
    all2.wait_recv()

    def gradients(here, cols, long, gated_back):
        return (
            (g_v[here, cols].astype(F32) * long).astype(BF16),
            (gated_back * conv[2, here, cols]).astype(BF16),
            (gated_back * conv[1, here, cols]).astype(BF16),
        )

    eye = jnp.where(
        lax.broadcasted_iota(jnp.int32, (16, B), 0) == lax.broadcasted_iota(jnp.int32, (16, B), 1),
        1.0, 0.0,
    ).astype(BF16)
    for tile in range(4):
        cols = slice(tile * B, tile * B + B)
        arrived = recv2[tile * 32 : tile * 32 + 32].astype(F32).reshape(2 * B, B).astype(BF16)
        head = lax.dot_general(
            eye, arrived, (((1,), (1,)), ((), ())), preferred_element_type=F32
        ).astype(BF16)
        head = dot(head, squares[6])
        for a, value in enumerate(gradients(slice(0, 16), cols, head[:, :B], head[:, B:])):
            halo2_s[a, :, cols] = value[0:8]

    halo2 = halo_copy(halo2_s, halo2_r, dma_sems.at[6], dma_sems.at[7], -1)

    @pl.when(me > 0)
    def _():
        halo2.start()

    @pl.loop(0, 4, unroll=2)
    def _(tile):
        cols = pl.ds(pl.multiple_of(tile * B, B), B)
        arrived = recv2[pl.ds(pl.multiple_of(tile * 32, 32), 32)].astype(F32).reshape(2 * B, B)
        rows = dot(arrived.T.astype(BF16), squares[6])
        long, gated_back = rows[:, :B], rows[:, B:]
        mixed_out[:, cols] = (conv[0, :, cols] * long).astype(BF16)
        for a, value in enumerate(gradients(slice(0, B), cols, long, gated_back)):
            ext_back[a, 0:B, cols] = value.astype(F32)

    def reverse(a, first_row, rows, cols):
        acc = taps[a, 0:1, cols] * ext_back[a, first_row : first_row + rows, cols]
        for j in range(1, TAPS):
            start = first_row + j
            acc = acc + taps[a, j : j + 1, cols] * ext_back[a, start : start + rows, cols]
        grads_out[a, first_row : first_row + rows, cols] = acc.astype(BF16)

    @pl.loop(0, 4)
    def _(tile):
        cols = pl.ds(pl.multiple_of(tile * B, B), B)
        for a in range(3):
            for first_row, rows in ((0, 32), (32, 32), (64, 32), (96, 16)):
                reverse(a, first_row, rows, cols)

    @pl.when(me < n - 1)
    def _():
        halo2.wait_recv()
        for a in range(3):
            ext_back[a, B : B + 8, :] = halo2_r[a].astype(F32)

    @pl.loop(0, 4, unroll=True)
    def _(tile):
        cols = pl.ds(pl.multiple_of(tile * B, B), B)
        for a in range(3):
            reverse(a, B - 16, 16, cols)

    @pl.when(me < n - 1)
    def _():
        halo1.wait_send()

    @pl.when(me > 0)
    def _():
        halo2.wait_send()

    all1.wait_send()
    all2.wait_send()


def store(mixed_in, grads_in, fgrad_in, mixed_out, grads_out, fgrad_out, sems):
    copies = [
        pltpu.make_async_copy(src, dst, sems.at[i])
        for i, (src, dst) in enumerate(
            [(grads_in, grads_out), (fgrad_in, fgrad_out), (mixed_in, mixed_out)]
        )
    ]
    for copy in copies:
        copy.start()
    for copy in copies:
        copy.wait()


def shards(query_proj, key_proj, value_proj, short_taps, long_filter, grad_mixed):
    rows, channels = query_proj.shape
    filt = long_filter.reshape(PER, B, B).transpose(1, 0, 2).reshape(PER * B, B)
    squares, twist = jnp.asarray(SQUARES), jnp.asarray(TWIST)
    operands = (query_proj, key_proj, value_proj, grad_mixed, short_taps, filt, squares, twist)
    operands = tuple(pltpu.with_memory_space_constraint(x, pltpu.HBM) for x in operands)
    tokens = pltpu.VMEM((rows, channels), BF16)
    edge = pltpu.VMEM((3, 8, channels), BF16)
    blocks = pltpu.VMEM((B, 8, B), BF16)
    tall = pltpu.VMEM((8 * B, B), F32)
    mid = pltpu.VMEM((12 * B, 2 * B), BF16)
    out_shape = (
        jax.ShapeDtypeStruct((rows, channels), BF16),
        jax.ShapeDtypeStruct((3, rows, channels), BF16),
        jax.ShapeDtypeStruct((PER * B, B), F32),
    )
    results = pl.pallas_call(
        kernel,
        name="hyena",
        out_shape=out_shape,
        in_specs=[pl.BlockSpec(memory_space=pl.ANY)] * len(operands),
        out_specs=[pl.BlockSpec(memory_space=pltpu.VMEM)] * 3,
        scratch_shapes=[
            tokens, tokens, tokens, tokens,
            pltpu.VMEM(short_taps.shape, F32),
            pltpu.VMEM(filt.shape, F32),
            pltpu.VMEM(squares.shape, BF16),
            pltpu.VMEM(twist.shape, F32),
            pltpu.VMEM((3, rows + 8, channels), F32),
            pltpu.VMEM((3, rows + 8, channels), F32),
            pltpu.VMEM((3, rows, channels), F32),
            edge, edge, edge, edge,
            pltpu.VMEM((rows, 2 * channels), BF16),
            blocks, blocks, blocks, blocks,
            tall, tall,
            mid, mid,
            pltpu.VMEM((12 * B, 2 * B), F32),
            mid, mid,
            pltpu.SemaphoreType.DMA((len(operands),)),
            pltpu.SemaphoreType.DMA((8,)),
            pltpu.SemaphoreType.REGULAR,
        ],
        compiler_params=pltpu.CompilerParams(collective_id=0, has_side_effects=True, vmem_limit_bytes=24 * 1024 * 1024),
    )(*operands)
    mixed, grads, fgrad = pl.pallas_call(
        store,
        name="store",
        out_shape=out_shape,
        in_specs=[pl.BlockSpec(memory_space=pltpu.VMEM)] * 3,
        out_specs=[pl.BlockSpec(memory_space=pl.ANY)] * 3,
        scratch_shapes=[pltpu.SemaphoreType.DMA((3,))],
        compiler_params=pltpu.CompilerParams(vmem_limit_bytes=2 * 1024 * 1024),
    )(*results)
    filter_grad = fgrad.reshape(B, PER, B).transpose(1, 0, 2).reshape(1, PER, SEQ)
    return (mixed, grads, filter_grad)


def solution(mesh):
    return jax.shard_map(
        shards,
        mesh=mesh,
        in_specs=(
            P("context", "tensor"),
            P("context", "tensor"),
            P("context", "tensor"),
            P(None, None, "tensor"),
            P("tensor", "context", None),
            P("context", "tensor"),
        ),
        out_specs=(
            P("context", "tensor"),
            P(None, "context", "tensor"),
            P("tensor", "context", None),
        ),
        check_vma=False,
    )
```
